128 devices in a mesh: row: 8 (over y, core), col: 16 (over x, z).
Axes of the slice: x: 4, y: 4, z: 4, core: 2. Of those that a mesh axis runs over, the one named last changes fastest.
Arguments:
- tensor_tiles: bfloat16 [512, 128, 128, 128], P(('row', 'col')), may hold values from -384 to 384
- tile_mode1: int32 [512], P(('row', 'col')), may hold values from 0 to 1023, as said below
- tile_mode2: int32 [512], P(('row', 'col')), may hold values from 0 to 127
- tile_mode3: int32 [512], P(('row', 'col')), may hold values from 0 to 63
- factor_mode2: bfloat16 [48, 16384], P(None, 'col'), may hold values from -1 to 1
- factor_mode3: bfloat16 [48, 8192], P(None, 'row'), may hold values from -1 to 1
Outputs:
- factor_mode1: float32 [48, 131072], P(None, ('row', 'col'))
The draws below stay inside these ranges and needn't reach their ends.
Inputs may be any that keep to these rules, and one draw needn't show every extreme that they name: `tile_mode1`: tiles at positions g*64 to (g+1)*64 - 1 have mode-1 blocks in g*128 to (g+1)*128 - 1; the 4 tiles at positions d*4 to (d+1)*4 - 1 have mode-1 blocks in distinct groups of 8 consecutive blocks (block // 8 all different).
All inputs are finite; a program needn't handle non-finite values.
Results may differ from the reference program's by a relative error of at most 0.0003.
Values may be sent and summed in bfloat16 or wider, within the bound.
No kernel may reach another device: no remote copies, remote signals or barrier semaphores. Data moves between devices by JAX's collectives and lax.ppermute only.
A program may use at most 128 MiB of HBM per device.

```python
import jax
import jax.numpy as jnp
from jax import lax

TS = 128
R = 48
TILES_DEV = 4
IB_DEV = 8
NI = 1024
NJ = 128
NK = 64
NTILES = 512
IB_ROW = 128
ROW_TILES = 64


def mixed_factor(key, row_count):
    key_noise, key_shared = jax.random.split(key)
    weight_mix = 1.0
    noise = jax.random.normal(key_noise, (R, row_count), jnp.float32)
    shared = jax.random.normal(key_shared, (row_count,), jnp.float32)
    combined = jnp.clip(noise, -4.0, 4.0) + jnp.clip(shared, -4.0, 4.0)[None, :]
    return (combined / jnp.sqrt((1.0 + weight_mix) * row_count)).astype(jnp.bfloat16)


def draw_factor_mode2(key, part):
    return mixed_factor(jax.random.fold_in(key, 2), NJ * TS)


def draw_factor_mode3(key, part):
    return mixed_factor(jax.random.fold_in(key, 3), NK * TS)


def draw_tile_mode1(key, part):
    positions = jnp.arange(NTILES, dtype=jnp.int32)
    col_count = ROW_TILES // TILES_DEV
    device_ids = positions // TILES_DEV
    within_dev = positions % TILES_DEV
    col_index = device_ids % col_count
    grid_row = device_ids // col_count
    bases = jax.random.randint(jax.random.fold_in(key, 1), (NTILES // TILES_DEV,), 0, col_count, dtype=jnp.int32)
    base_of = bases[device_ids]
    base_of = jnp.where(col_index == 0, 0, jnp.where(col_index == col_count - 1, col_count - 1, base_of))
    owners = (base_of + within_dev) % col_count
    offsets = jax.random.randint(jax.random.fold_in(key, 4), (NTILES,), 0, IB_DEV, dtype=jnp.int32)
    first_low = (within_dev == 0) & (col_index == 0)
    first_high = (within_dev == 0) & (col_index == col_count - 1)
    offsets = jnp.where(first_low, 0, jnp.where(first_high, IB_DEV - 1, offsets))
    return (grid_row * IB_ROW + owners * IB_DEV + offsets).astype(jnp.int32)


def place_ends(drawn, key, smallest, top_value):
    place = [jax.random.randint(jax.random.fold_in(key, axis), (), 0, length) for axis, length in enumerate(drawn.shape)]
    widest = drawn.shape.index(max(drawn.shape))
    beside = place[:widest] + [(place[widest] + 1) % drawn.shape[widest]] + place[widest + 1:]
    return drawn.at[tuple(place)].set(smallest).at[tuple(beside)].set(top_value)


def level_of(stream_key, extent, cuts, least, largest):
    gain, own = 1.0, jax.random.fold_in(stream_key, 6)
    for position, shards_of in cuts:
        steps = jnp.exp(jax.random.uniform(jax.random.fold_in(own, position), (shards_of,), jnp.float32, least / len(cuts), largest / len(cuts)))
        gain = gain * jnp.repeat(steps, extent[position] // shards_of).reshape([-1 if axis == position else 1 for axis in range(len(extent))])
    return gain


def centred(key, extent, spread, most, shards=(), kind=jnp.bfloat16):
    level = level_of(key, extent, shards, -0.22, 0.18) if shards else 1.0
    array = jax.random.normal(key, extent, jnp.float32) * spread * level
    return jnp.minimum(jnp.maximum(array, -most), most).astype(kind)


def setup_inputs(seed: int = 0) -> dict:
    splits = jax.random.split(jax.random.key(seed), 7)
    return {
        "tensor_tiles": centred(splits[0], (NTILES, TS, TS, TS), (0.5 * TS), 384.0, ((0, 128),)),
        "tile_mode1": draw_tile_mode1(jax.random.fold_in(splits[6], 71), 0),
        "tile_mode2": place_ends(jax.random.randint(splits[2], (NTILES,), 0, NJ), jax.random.fold_in(splits[2], 1), 0, NJ - 1).astype(jnp.int32),
        "tile_mode3": place_ends(jax.random.randint(splits[3], (NTILES,), 0, NK), jax.random.fold_in(splits[3], 1), 0, NK - 1).astype(jnp.int32),
        "factor_mode2": draw_factor_mode2(jax.random.fold_in(splits[6], 71), 0),
        "factor_mode3": draw_factor_mode3(jax.random.fold_in(splits[6], 71), 0),
    }


ridge_term = 0.5

def reference(tensor_tiles, tile_mode1, tile_mode2, tile_mode3, factor_mode2, factor_mode3):
    rank_count = factor_mode2.shape[0]
    gram_two = jnp.dot(factor_mode2.astype(jnp.float32), factor_mode2.T.astype(jnp.float32), preferred_element_type=jnp.float32)
    gram_three = jnp.dot(factor_mode3.astype(jnp.float32), factor_mode3.T.astype(jnp.float32), preferred_element_type=jnp.float32)
    system = gram_two * gram_three + ridge_term * jnp.eye(rank_count, dtype=jnp.float32)
    blocks_two = factor_mode2.reshape(rank_count, NJ, TS)
    blocks_three = factor_mode3.reshape(rank_count, NK, TS)

    def add_tile(accumulated, tile_item):
        one_tile, index_one, index_two, index_three = tile_item
        rows_two = lax.dynamic_index_in_dim(blocks_two, index_two, 1, keepdims=False).astype(jnp.float32)
        rows_three = lax.dynamic_index_in_dim(blocks_three, index_three, 1, keepdims=False).astype(jnp.float32)
        contracted = jnp.einsum('rc,abc->rab', rows_three, one_tile.astype(jnp.float32), precision=lax.Precision.HIGHEST)
        tile_rows = jnp.einsum('rab,rb->ra', contracted, rows_two, precision=lax.Precision.HIGHEST)
        column_start = (index_one * TS).astype(jnp.int32)
        anchor = jnp.zeros((), jnp.int32)
        current = lax.dynamic_slice(accumulated, (anchor, column_start), (rank_count, TS))
        return (lax.dynamic_update_slice(accumulated, current + tile_rows, (anchor, column_start)), None)
    initial = jnp.zeros((rank_count, NI * TS), jnp.float32)
    right_side, _ = lax.scan(add_tile, initial, (tensor_tiles, tile_mode1, tile_mode2, tile_mode3))
    cholesky_factor = jnp.linalg.cholesky(system)
    middle = lax.linalg.triangular_solve(cholesky_factor, right_side, left_side=True, lower=True)
    return lax.linalg.triangular_solve(cholesky_factor, middle, left_side=True, lower=True, transpose_a=True)
```

```python
import jax
import jax.numpy as jnp
from jax import lax
from jax.experimental import pallas as pl
from jax.experimental.pallas import tpu as pltpu
from jax.sharding import PartitionSpec as P

IB_DEV = 8
META = 8

ridge_term = 0.5

F32 = jnp.float32
BF16 = jnp.bfloat16
VMEM = pl.BlockSpec(memory_space=pltpu.VMEM)
SMEM = pl.BlockSpec(memory_space=pltpu.SMEM)
MIB = 1 << 20


def first_kernel(mode3_ref, three_ref, tiles_ref, out_ref, weight_ref):
    rank = three_ref.shape[1]
    edge = tiles_ref.shape[3]
    per_owner = three_ref.shape[2] // edge
    pair = pl.program_id(0)

    @pl.when(pl.program_id(1) == 0)
    def _():
        weight_ref[...] = jnp.zeros_like(weight_ref)
        for side in range(2):
            block = mode3_ref[2 * pair + side]
            start = pl.multiple_of(lax.rem(block, per_owner) * edge, edge)
            rows = three_ref[lax.div(block, per_owner), :, pl.ds(start, edge)]
            weight_ref[side * rank : (side + 1) * rank, side * edge : (side + 1) * edge] = rows

    both = jnp.concatenate([tiles_ref[0, 0], tiles_ref[0, 1]], axis=-1)
    out_ref[0] = lax.dot_general(
        both, weight_ref[...], (((1,), (1,)), ((), ())), preferred_element_type=F32
    )


def contract_first(mode3, three, tiles):
    tile_count, edge = tiles.shape[0], tiles.shape[1]
    pairs = tile_count // 2
    rows = edge * edge
    step = 4096
    tiles = tiles.reshape(pairs, 2, rows, edge)
    return pl.pallas_call(
        first_kernel,
        grid=(pairs, rows // step),
        in_specs=[
            SMEM,
            VMEM,
            pl.BlockSpec((1, 2, step, edge), lambda p, s: (p, 0, s, 0)),
        ],
        out_specs=pl.BlockSpec((1, step, 128), lambda p, s: (p, s, 0)),
        out_shape=jax.ShapeDtypeStruct((pairs, rows, 128), F32),
        scratch_shapes=[pltpu.VMEM((128, 2 * edge), BF16)],
        compiler_params=pltpu.CompilerParams(vmem_limit_bytes=14 * MIB),
        cost_estimate=pl.CostEstimate(
            flops=2 * pairs * rows * 256 * 256, bytes_accessed=40 * MIB, transcendentals=0
        ),
        name="contract_first",
    )(mode3, three, tiles)


def half_rows(own, other, first):
    low = jnp.where(first, own, other)
    high = jnp.where(first, other, own)
    return low, high


def second_kernel(mode1_ref, mode2_ref, core_ref, mid_ref, own_ref, other_ref, send_ref, row_ref):
    owners, half, width = own_ref.shape
    rank = 2 * half
    edge = send_ref.shape[2]
    per_owner = width // edge
    pairs = mid_ref.shape[0]
    first = core_ref[0] == 0
    send_ref[...] = jnp.zeros_like(send_ref)
    for pair in range(pairs):
        parts = []
        for side in range(2):
            block = mode2_ref[2 * pair + side]
            start = pl.multiple_of(lax.rem(block, per_owner) * edge, edge)
            owner = lax.div(block, per_owner)
            own = own_ref[owner, :, pl.ds(start, edge)].astype(F32)
            other = other_ref[owner, :, pl.ds(start, edge)].astype(F32)
            parts.extend(half_rows(own, other, first))
        parts.append(jnp.zeros((128 - 2 * rank, edge), F32))
        factor = jnp.concatenate(parts, axis=0).T.reshape(1, edge // 8, 8, 128)

        @pl.loop(0, edge // 8)
        def _(group):
            start = pl.multiple_of(group * 8 * edge, 8 * edge)
            block = mid_ref[pair, pl.ds(start, 8 * edge), :].reshape(8, edge // 8, 8, 128)
            summed = jnp.sum(block * factor, axis=1)
            row_ref[pl.ds(pl.multiple_of(group * 8, 8), 8), :] = jnp.sum(summed, axis=1)

        flipped = row_ref[...].T
        for side in range(2):
            block = mode1_ref[2 * pair + side]
            slot = lax.rem(lax.div(block, IB_DEV), owners)
            offset = lax.rem(block, IB_DEV).astype(F32)
            send_ref[slot, 0:rank, :] = flipped[side * rank : (side + 1) * rank, :]
            send_ref[slot, rank : rank + META, :] = jnp.full((META, edge), offset, F32)


def contract_second(mode1, mode2, core, mid, own, other):
    owners, half, _ = own.shape
    return pl.pallas_call(
        second_kernel,
        in_specs=[SMEM, SMEM, SMEM, VMEM, VMEM, VMEM],
        out_specs=VMEM,
        out_shape=jax.ShapeDtypeStruct((owners, 2 * half + META, 128), F32),
        scratch_shapes=[pltpu.VMEM((128, 128), F32)],
        compiler_params=pltpu.CompilerParams(vmem_limit_bytes=24 * MIB),
        cost_estimate=pl.CostEstimate(flops=8 * MIB, bytes_accessed=20 * MIB, transcendentals=0),
        name="contract_second",
    )(mode1, mode2, core, mid, own, other)


def inverse_kernel(core_ref, own_ref, other_ref, three_ref, out_ref):
    owners, half, _ = own_ref.shape
    rank = 2 * half
    first = core_ref[0] == 0
    contract = (((1,), (1,)), ((), ()))
    gram_two = jnp.zeros((rank, rank), F32)
    for owner in range(owners):
        low, high = half_rows(own_ref[owner].astype(F32), other_ref[owner].astype(F32), first)
        rows = jnp.concatenate([low, high], axis=0).astype(BF16)
        gram_two += lax.dot_general(rows, rows, contract, preferred_element_type=F32)
    gram_three = jnp.zeros((rank, rank), F32)
    for owner in range(three_ref.shape[0]):
        rows = three_ref[owner]
        gram_three += lax.dot_general(rows, rows, contract, preferred_element_type=F32)
    row_ids = lax.broadcasted_iota(jnp.int32, (rank, rank), 0)
    col_ids = lax.broadcasted_iota(jnp.int32, (rank, rank), 1)
    unit = (row_ids == col_ids).astype(F32)
    system = gram_two * gram_three + ridge_term * unit
    work = jnp.concatenate([system, unit, jnp.zeros((rank, 128 - 2 * rank), F32)], axis=1)
    below = lax.broadcasted_iota(jnp.int32, (rank, 128), 0)
    scale = jnp.zeros((rank, 128), F32)
    for k in range(rank):
        pivot_row = work[k : k + 1, :]
        inverse = 1.0 / pivot_row[:, k : k + 1]
        scale = jnp.where(below == k, inverse, scale)
        factor = jnp.where(below > k, work[:, k : k + 1] * inverse, 0.0)
        work = work - factor * pivot_row
    lower = work[:, rank : 2 * rank]
    out_ref[...] = lax.dot_general(
        lower,
        lower * scale[:, :rank],
        (((0,), (0,)), ((), ())),
        precision=lax.Precision.HIGHEST,
        preferred_element_type=F32,
    )


def system_inverse(core, own, other, three):
    rank = three.shape[1]
    return pl.pallas_call(
        inverse_kernel,
        in_specs=[SMEM, VMEM, VMEM, VMEM],
        out_specs=VMEM,
        out_shape=jax.ShapeDtypeStruct((rank, rank), F32),
        compiler_params=pltpu.CompilerParams(vmem_limit_bytes=16 * MIB),
        cost_estimate=pl.CostEstimate(flops=8 * MIB, bytes_accessed=16 * MIB, transcendentals=0),
        name="system_inverse",
    )(core, own, other, three)


def solve_kernel(received_ref, inverse_ref, out_ref, side_ref):
    owners, _, edge = received_ref.shape
    rank = inverse_ref.shape[0]
    for offset in range(IB_DEV):
        total = jnp.zeros((rank // 8, 8, edge), F32)
        for owner in range(owners):
            hit = (received_ref[owner, rank : rank + META, :] == float(offset))[None]
            rows = received_ref[owner, 0:rank, :].reshape(rank // 8, 8, edge)
            total += jnp.where(hit, rows, 0.0)
        side_ref[:, offset * edge : (offset + 1) * edge] = total.reshape(rank, edge)
    out_ref[...] = jnp.dot(
        inverse_ref[...],
        side_ref[...],
        precision=lax.Precision.HIGHEST,
        preferred_element_type=F32,
    )


def solve(received, inverse):
    rank = inverse.shape[0]
    edge = received.shape[2]
    return pl.pallas_call(
        solve_kernel,
        in_specs=[VMEM, VMEM],
        out_specs=VMEM,
        out_shape=jax.ShapeDtypeStruct((rank, IB_DEV * edge), F32),
        scratch_shapes=[pltpu.VMEM((rank, IB_DEV * edge), F32)],
        compiler_params=pltpu.CompilerParams(vmem_limit_bytes=16 * MIB),
        name="solve",
    )(received, inverse)


def body(tensor_tiles, tile_mode1, tile_mode2, tile_mode3, factor_mode2, factor_mode3):
    rank, width = factor_mode2.shape
    half = rank // 2
    cols = lax.axis_size("col")
    core = lax.rem(lax.axis_index("row"), 2).astype(jnp.int32)
    mine = lax.dynamic_slice_in_dim(factor_mode2, core * half, half, 0)
    own = lax.all_to_all(
        jnp.broadcast_to(mine[None], (cols, half, width)), "col", 0, 0, tiled=True
    )
    three = lax.all_gather(factor_mode3, "row", axis=0, tiled=False)
    mid = contract_first(tile_mode3, three, tensor_tiles)
    swap = [(i, i ^ 1) for i in range(lax.axis_size("row"))]
    other = lax.ppermute(own, "row", swap)
    core_id = core[None]
    send = contract_second(tile_mode1, tile_mode2, core_id, mid, own, other)
    received = lax.all_to_all(send, "col", 0, 0, tiled=True)
    inverse = system_inverse(core_id, own, other, three)
    return solve(received, inverse)


def solution(mesh):
    in_specs = (
        P(("row", "col"), None, None, None),
        P(("row", "col")),
        P(("row", "col")),
        P(("row", "col")),
        P(None, "col"),
        P(None, "row"),
    )
    out_specs = P(None, ("row", "col"))
    return jax.shard_map(body, mesh=mesh, in_specs=in_specs, out_specs=out_specs, check_vma=False)
```

```python
import jax
import jax.numpy as jnp
from jax import lax
from jax.experimental import pallas as pl
from jax.experimental.pallas import tpu as pltpu
from jax.sharding import PartitionSpec as P


IB_DEV = 8
META = 8

ridge_term = 0.5

F32 = jnp.float32
BF16 = jnp.bfloat16
VMEM = pl.BlockSpec(memory_space=pltpu.VMEM)
HBM = pl.BlockSpec(memory_space=pltpu.HBM)
SMEM = pl.BlockSpec(memory_space=pltpu.SMEM)
MIB = 1 << 20


CHUNKS = 4
EARLY = 2
DEPTH = 3
PARTS = 2


def early_kernel(tiles_ref, out_ref, sems):
    step = out_ref.shape[2]
    copies = [
        pltpu.make_async_copy(
            tiles_ref.at[side, pl.ds(chunk * step, step)],
            out_ref.at[side, chunk],
            sems.at[side, chunk],
        )
        for chunk in range(EARLY)
        for side in range(2)
    ]
    for copy in copies:
        copy.start()
    for copy in copies:
        copy.wait()


def fetch_early(tiles):
    edge = tiles.shape[1]
    return pl.pallas_call(
        early_kernel,
        in_specs=[HBM],
        out_specs=VMEM,
        out_shape=jax.ShapeDtypeStruct((2, EARLY, edge // CHUNKS, edge, edge), BF16),
        scratch_shapes=[pltpu.SemaphoreType.DMA((2, EARLY))],
        compiler_params=pltpu.CompilerParams(vmem_limit_bytes=8 * MIB),
        cost_estimate=pl.CostEstimate(flops=0, bytes_accessed=8 * MIB, transcendentals=0),
        name="fetch_early",
    )(tiles)


def half_rows(own, other, first):
    low = jnp.where(first, own, other)
    high = jnp.where(first, other, own)
    return low, high


def near_slot(row, owner, chips):
    distance = lax.rem(lax.div(row, 2) - lax.div(owner, 2) + chips, chips)
    return distance + chips * lax.rem(row + owner, 2)


def rows_kernel(
    mode1_ref,
    mode2_ref,
    mode3_ref,
    row_id_ref,
    own_ref,
    other_ref,
    three_ref,
    early_ref,
    tiles_ref,
    send_ref,
    weight_ref,
    tile_ref,
    row_ref,
    sems,
):
    tile_count, edge = tiles_ref.shape[:2]
    step = edge // CHUNKS
    steps = [(pair, chunk) for pair in range(tile_count // 2) for chunk in range(CHUNKS)]
    late = steps[EARLY:]

    def copies(number):
        pair, chunk = late[number]
        return [
            pltpu.make_async_copy(
                tiles_ref.at[2 * pair + side, pl.ds(chunk * step, step)],
                tile_ref.at[number, side],
                sems.at[number, side],
            )
            for side in range(2)
        ]

    for number in range(DEPTH):
        for copy in copies(number):
            copy.start()

    @pl.when(row_id_ref[0] >= 0)
    def _():
        fill_rows(
            mode1_ref,
            mode2_ref,
            mode3_ref,
            row_id_ref,
            own_ref,
            other_ref,
            three_ref,
            early_ref,
            send_ref,
            weight_ref,
            tile_ref,
            row_ref,
            steps,
            late,
            copies,
        )


def fill_rows(
    mode1_ref,
    mode2_ref,
    mode3_ref,
    row_id_ref,
    own_ref,
    other_ref,
    three_ref,
    early_ref,
    send_ref,
    weight_ref,
    tile_ref,
    row_ref,
    steps,
    late,
    copies,
):
    owners, half, width = own_ref.shape
    rank = 2 * half
    edge = tile_ref.shape[-1]
    step = tile_ref.shape[2]
    pairs = weight_ref.shape[0]
    per_owner = width // edge

    def place(block):
        start = pl.multiple_of(lax.rem(block, per_owner) * edge, edge)
        return lax.div(block, per_owner), pl.ds(start, edge)

    first = lax.rem(row_id_ref[0], 2) == 0
    send_ref[...] = jnp.zeros_like(send_ref)
    weight_ref[...] = jnp.zeros_like(weight_ref)
    factors = []
    for pair in range(pairs):
        parts = []
        for side in range(2):
            owner, span = place(mode3_ref[2 * pair + side])
            owner = near_slot(row_id_ref[0], owner, three_ref.shape[0] // 2)
            weight_ref[pair, side * rank : (side + 1) * rank, side * edge : (side + 1) * edge] = (
                three_ref[owner, :, span]
            )
            owner, span = place(mode2_ref[2 * pair + side])
            own = own_ref[owner, :, span].astype(F32)
            other = other_ref[owner, :, span].astype(F32)
            parts.extend(half_rows(own, other, first))
        parts.append(jnp.zeros((128 - 2 * rank, edge), F32))
        factors.append(jnp.concatenate(parts, axis=0).T.reshape(1, edge // 8, 8, 128))

    part = step // PARTS
    for number, (pair, chunk) in enumerate(steps):
        if number >= EARLY:
            late_number = number - EARLY
            for copy in copies(late_number):
                copy.wait()
            if late_number + DEPTH < len(late):
                for copy in copies(late_number + DEPTH):
                    copy.start()
        for index in range(PARTS):
            inner = slice(index * part, (index + 1) * part)
            if number < EARLY:
                sides = [early_ref[side, chunk, inner] for side in range(2)]
            else:
                sides = [tile_ref[late_number, side, inner] for side in range(2)]
            both = jnp.concatenate(sides, axis=-1).reshape(part * edge, 2 * edge)
            mid = lax.dot_general(
                both, weight_ref[pair], (((1,), (1,)), ((), ())), preferred_element_type=F32
            )
            terms = mid.reshape(part, edge // 8, 8, 128) * factors[pair]
            while terms.shape[1] > 1:
                terms = terms.reshape(part, terms.shape[1] // 2, 2, 8, 128)
                terms = terms[:, :, 0] + terms[:, :, 1]
            start = chunk * step + index * part
            row_ref[start : start + part, :] = jnp.sum(terms.reshape(part, 8, 128), axis=1)
        if chunk == CHUNKS - 1:
            flipped = row_ref[...].T
            for side in range(2):
                block = mode1_ref[2 * pair + side]
                slot = lax.rem(lax.div(block, IB_DEV), owners)
                offset = lax.rem(block, IB_DEV).astype(F32)
                send_ref[slot, 0:rank, :] = flipped[side * rank : (side + 1) * rank, :]
                send_ref[slot, rank : rank + META, :] = jnp.full((META, edge), offset, F32)


def tile_rows(mode1, mode2, mode3, row, own, other, three, early, tiles):
    owners, half, _ = own.shape
    tile_count, edge = tiles.shape[:2]
    late = tile_count // 2 * CHUNKS - EARLY
    return pl.pallas_call(
        rows_kernel,
        in_specs=[SMEM] * 4 + [VMEM] * 4 + [HBM],
        out_specs=VMEM,
        out_shape=jax.ShapeDtypeStruct((owners, 2 * half + META, edge), F32),
        scratch_shapes=[
            pltpu.VMEM((tile_count // 2, 128, 2 * edge), BF16),
            pltpu.VMEM((late, 2, edge // CHUNKS, edge, edge), BF16),
            pltpu.VMEM((edge, 128), F32),
            pltpu.SemaphoreType.DMA((late, 2)),
        ],
        compiler_params=pltpu.CompilerParams(vmem_limit_bytes=32 * MIB),
        cost_estimate=pl.CostEstimate(
            flops=tile_count * edge * edge * 256 * 256, bytes_accessed=16 * MIB, transcendentals=0
        ),
        name="tile_rows",
    )(mode1, mode2, mode3, row, own, other, three, early, tiles)


def inverse_kernel(row_id_ref, own_ref, other_ref, three_ref, out_ref):
    owners, half, _ = own_ref.shape
    rank = 2 * half
    first = lax.rem(row_id_ref[0], 2) == 0
    contract = (((1,), (1,)), ((), ()))
    gram_two = jnp.zeros((rank, rank), F32)
    for owner in range(owners):
        low, high = half_rows(own_ref[owner].astype(F32), other_ref[owner].astype(F32), first)
        rows = jnp.concatenate([low, high], axis=0).astype(BF16)
        gram_two += lax.dot_general(rows, rows, contract, preferred_element_type=F32)
    gram_three = jnp.zeros((rank, rank), F32)
    for owner in range(three_ref.shape[0]):
        rows = three_ref[owner]
        gram_three += lax.dot_general(rows, rows, contract, preferred_element_type=F32)
    row_ids = lax.broadcasted_iota(jnp.int32, (rank, rank), 0)
    col_ids = lax.broadcasted_iota(jnp.int32, (rank, rank), 1)
    unit = (row_ids == col_ids).astype(F32)
    system = gram_two * gram_three + ridge_term * unit
    work = jnp.concatenate([system, unit, jnp.zeros((rank, 128 - 2 * rank), F32)], axis=1)
    below = lax.broadcasted_iota(jnp.int32, (rank, 128), 0)
    scale = jnp.zeros((rank, 128), F32)
    for k in range(rank):
        pivot_row = work[k : k + 1, :]
        inverse = 1.0 / pivot_row[:, k : k + 1]
        scale = jnp.where(below == k, inverse, scale)
        factor = jnp.where(below > k, work[:, k : k + 1] * inverse, 0.0)
        work = work - factor * pivot_row
    lower = work[:, rank : 2 * rank]
    out_ref[...] = lax.dot_general(
        lower,
        lower * scale[:, :rank],
        (((0,), (0,)), ((), ())),
        precision=lax.Precision.HIGHEST,
        preferred_element_type=F32,
    )


def system_inverse(row, own, other, three):
    rank = three.shape[1]
    return pl.pallas_call(
        inverse_kernel,
        in_specs=[SMEM, VMEM, VMEM, VMEM],
        out_specs=VMEM,
        out_shape=jax.ShapeDtypeStruct((rank, rank), F32),
        compiler_params=pltpu.CompilerParams(vmem_limit_bytes=16 * MIB),
        cost_estimate=pl.CostEstimate(flops=8 * MIB, bytes_accessed=16 * MIB, transcendentals=0),
        name="system_inverse",
    )(row, own, other, three)


def solve_kernel(received_ref, inverse_ref, out_ref, side_ref):
    owners, _, edge = received_ref.shape
    rank = inverse_ref.shape[0]
    for offset in range(IB_DEV):
        total = jnp.zeros((rank // 8, 8, edge), F32)
        for owner in range(owners):
            hit = (received_ref[owner, rank : rank + META, :] == float(offset))[None]
            rows = received_ref[owner, 0:rank, :].reshape(rank // 8, 8, edge)
            total += jnp.where(hit, rows, 0.0)
        side_ref[:, offset * edge : (offset + 1) * edge] = total.reshape(rank, edge)
    out_ref[...] = jnp.dot(
        inverse_ref[...],
        side_ref[...],
        precision=lax.Precision.HIGHEST,
        preferred_element_type=F32,
    )


def solve(received, inverse):
    rank = inverse.shape[0]
    edge = received.shape[2]
    return pl.pallas_call(
        solve_kernel,
        in_specs=[VMEM, VMEM],
        out_specs=VMEM,
        out_shape=jax.ShapeDtypeStruct((rank, IB_DEV * edge), F32),
        scratch_shapes=[pltpu.VMEM((rank, IB_DEV * edge), F32)],
        compiler_params=pltpu.CompilerParams(vmem_limit_bytes=16 * MIB),
        name="solve",
    )(received, inverse)


def update(tensor_tiles, tile_mode1, tile_mode2, tile_mode3, factor_mode2, factor_mode3):
    rank, width = factor_mode2.shape
    half = rank // 2
    cols = lax.axis_size("col")
    row = lax.axis_index("row").astype(jnp.int32)
    core = lax.rem(row, 2)
    mine = jnp.where(core == 0, factor_mode2[:half], factor_mode2[half:])
    tiles = pltpu.with_memory_space_constraint(tensor_tiles, pltpu.HBM)
    own = lax.all_to_all(jnp.broadcast_to(mine[None], (cols, half, width)), "col", 0, 0, tiled=True)
    devices = lax.axis_size("row")
    chips = devices // 2
    near, far = [factor_mode3], []
    for distance in range(1, chips):
        shift = [(i, (i + 2 * distance) % devices) for i in range(devices)]
        near.append(lax.ppermute(factor_mode3, "row", shift))
    for distance in range(chips):
        swap = [(i, i ^ 1) for i in range(devices)]
        far.append(lax.ppermute(near[distance], "row", swap))
    three = jnp.stack(near + far)
    swap = [(i, i ^ 1) for i in range(lax.axis_size("row"))]
    other = lax.ppermute(own, "row", swap)
    early = fetch_early(tiles)
    row_id = row[None]
    send = tile_rows(tile_mode1, tile_mode2, tile_mode3, row_id, own, other, three, early, tiles)
    received = lax.all_to_all(send, "col", 0, 0, tiled=True)
    inverse = system_inverse(row_id, own, other, three)
    return solve(received, inverse)


def solution(mesh):
    in_specs = (
        P(("row", "col"), None, None, None),
        P(("row", "col")),
        P(("row", "col")),
        P(("row", "col")),
        P(None, "col"),
        P(None, "row"),
    )
    out_specs = P(None, ("row", "col"))
    return jax.shard_map(update, mesh=mesh, in_specs=in_specs, out_specs=out_specs, check_vma=False)
```

```python
import jax
import jax.numpy as jnp
from jax import lax
from jax.experimental import pallas as pl
from jax.experimental.pallas import tpu as pltpu
from jax.sharding import PartitionSpec as P


IB_DEV = 8
META = 8

ridge_term = 0.5

F32 = jnp.float32
BF16 = jnp.bfloat16
VMEM = pl.BlockSpec(memory_space=pltpu.VMEM)
HBM = pl.BlockSpec(memory_space=pltpu.HBM)
SMEM = pl.BlockSpec(memory_space=pltpu.SMEM)
MIB = 1 << 20


CHUNKS = 4
EARLY = 2
DEPTH = 3
PARTS = 2


def early_kernel(tiles_ref, out_ref, sems):
    step = out_ref.shape[2]
    copies = [
        pltpu.make_async_copy(
            tiles_ref.at[side, pl.ds(chunk * step, step)],
            out_ref.at[side, chunk],
            sems.at[side, chunk],
        )
        for chunk in range(EARLY)
        for side in range(2)
    ]
    for copy in copies:
        copy.start()
    for copy in copies:
        copy.wait()


def fetch_early(tiles):
    edge = tiles.shape[1]
    return pl.pallas_call(
        early_kernel,
        in_specs=[HBM],
        out_specs=VMEM,
        out_shape=jax.ShapeDtypeStruct((2, EARLY, edge // CHUNKS, edge, edge), BF16),
        scratch_shapes=[pltpu.SemaphoreType.DMA((2, EARLY))],
        compiler_params=pltpu.CompilerParams(vmem_limit_bytes=8 * MIB),
        cost_estimate=pl.CostEstimate(flops=0, bytes_accessed=8 * MIB, transcendentals=0),
        name="fetch_early",
    )(tiles)


def half_rows(own, other, first):
    low = jnp.where(first, own, other)
    high = jnp.where(first, other, own)
    return low, high


def near_slot(row, owner, chips):
    distance = lax.rem(lax.div(row, 2) - lax.div(owner, 2) + chips, chips)
    return distance + chips * lax.rem(row + owner, 2)


def rows_kernel(
    mode1_ref,
    mode2_ref,
    mode3_ref,
    row_id_ref,
    own_ref,
    other_ref,
    three_ref,
    early_ref,
    tiles_ref,
    send_ref,
    weight_ref,
    tile_ref,
    row_ref,
    sems,
):
    tile_count, edge = tiles_ref.shape[:2]
    step = edge // CHUNKS
    steps = [(pair, chunk) for pair in range(tile_count // 2) for chunk in range(CHUNKS)]
    late = steps[EARLY:]

    def copies(number):
        pair, chunk = late[number]
        return [
            pltpu.make_async_copy(
                tiles_ref.at[2 * pair + side, pl.ds(chunk * step, step)],
                tile_ref.at[number, side],
                sems.at[number, side],
            )
            for side in range(2)
        ]

    for number in range(DEPTH):
        for copy in copies(number):
            copy.start()

    @pl.when(row_id_ref[0] >= 0)
    def _():
        fill_rows(
            mode1_ref,
            mode2_ref,
            mode3_ref,
            row_id_ref,
            own_ref,
            other_ref,
            three_ref,
            early_ref,
            send_ref,
            weight_ref,
            tile_ref,
            row_ref,
            steps,
            late,
            copies,
        )


def fill_rows(
    mode1_ref,
    mode2_ref,
    mode3_ref,
    row_id_ref,
    own_ref,
    other_ref,
    three_ref,
    early_ref,
    send_ref,
    weight_ref,
    tile_ref,
    row_ref,
    steps,
    late,
    copies,
):
    owners, half, width = own_ref.shape
    rank = 2 * half
    edge = tile_ref.shape[-1]
    step = tile_ref.shape[2]
    pairs = weight_ref.shape[0]
    per_owner = width // edge

    def place(block):
        start = pl.multiple_of(lax.rem(block, per_owner) * edge, edge)
        return lax.div(block, per_owner), pl.ds(start, edge)

    first = lax.rem(row_id_ref[0], 2) == 0
    send_ref[...] = jnp.zeros_like(send_ref)
    weight_ref[...] = jnp.zeros_like(weight_ref)
    factors = []
    for pair in range(pairs):
        parts = []
        for side in range(2):
            owner, span = place(mode3_ref[2 * pair + side])
            owner = near_slot(row_id_ref[0], owner, three_ref.shape[0] // 2)
            weight_ref[pair, side * rank : (side + 1) * rank, side * edge : (side + 1) * edge] = (
                three_ref[owner, :, span]
            )
            owner, span = place(mode2_ref[2 * pair + side])
            own = own_ref[owner, :, span].astype(F32)
            other = other_ref[owner, :, span].astype(F32)
            parts.extend(half_rows(own, other, first))
        parts.append(jnp.zeros((128 - 2 * rank, edge), F32))
        factors.append(jnp.concatenate(parts, axis=0).T.reshape(1, edge // 8, 8, 128))

    part = step // PARTS
    for number, (pair, chunk) in enumerate(steps):
        if number >= EARLY:
            late_number = number - EARLY
            for copy in copies(late_number):
                copy.wait()
            if late_number + DEPTH < len(late):
                for copy in copies(late_number + DEPTH):
                    copy.start()
        for index in range(PARTS):
            inner = slice(index * part, (index + 1) * part)
            if number < EARLY:
                sides = [early_ref[side, chunk, inner] for side in range(2)]
            else:
                sides = [tile_ref[late_number, side, inner] for side in range(2)]
            both = jnp.concatenate(sides, axis=-1).reshape(part * edge, 2 * edge)
            mid = lax.dot_general(
                both, weight_ref[pair], (((1,), (1,)), ((), ())), preferred_element_type=F32
            )
            terms = mid.reshape(part, edge // 8, 8, 128) * factors[pair]
            while terms.shape[1] > 1:
                terms = terms.reshape(part, terms.shape[1] // 2, 2, 8, 128)
                terms = terms[:, :, 0] + terms[:, :, 1]
            start = chunk * step + index * part
            row_ref[start : start + part, :] = jnp.sum(terms.reshape(part, 8, 128), axis=1)
        if chunk == CHUNKS - 1:
            flipped = row_ref[...].T
            for side in range(2):
                block = mode1_ref[2 * pair + side]
                slot = lax.rem(lax.div(block, IB_DEV), owners)
                offset = lax.rem(block, IB_DEV).astype(F32)
                rows = flipped[side * rank : (side + 1) * rank, :]
                high = rows.astype(BF16)
                send_ref[slot, 0:rank, :] = high
                send_ref[slot, rank : 2 * rank, :] = (rows - high.astype(F32)).astype(BF16)
                send_ref[slot, 2 * rank : 2 * rank + META, :] = jnp.full(
                    (META, edge), offset, F32
                ).astype(BF16)


def tile_rows(mode1, mode2, mode3, row, own, other, three, early, tiles):
    owners, half, _ = own.shape
    tile_count, edge = tiles.shape[:2]
    late = tile_count // 2 * CHUNKS - EARLY
    return pl.pallas_call(
        rows_kernel,
        in_specs=[SMEM] * 4 + [VMEM] * 4 + [HBM],
        out_specs=VMEM,
        out_shape=jax.ShapeDtypeStruct((owners, 4 * half + META, edge), BF16),
        scratch_shapes=[
            pltpu.VMEM((tile_count // 2, 128, 2 * edge), BF16),
            pltpu.VMEM((late, 2, edge // CHUNKS, edge, edge), BF16),
            pltpu.VMEM((edge, 128), F32),
            pltpu.SemaphoreType.DMA((late, 2)),
        ],
        compiler_params=pltpu.CompilerParams(vmem_limit_bytes=32 * MIB),
        cost_estimate=pl.CostEstimate(
            flops=tile_count * edge * edge * 256 * 256, bytes_accessed=16 * MIB, transcendentals=0
        ),
        name="tile_rows",
    )(mode1, mode2, mode3, row, own, other, three, early, tiles)


def inverse_kernel(row_id_ref, own_ref, other_ref, three_ref, out_ref):
    owners, half, _ = own_ref.shape
    rank = 2 * half
    first = lax.rem(row_id_ref[0], 2) == 0
    contract = (((1,), (1,)), ((), ()))
    gram_two = jnp.zeros((rank, rank), F32)
    for owner in range(owners):
        low, high = half_rows(own_ref[owner].astype(F32), other_ref[owner].astype(F32), first)
        rows = jnp.concatenate([low, high], axis=0).astype(BF16)
        gram_two += lax.dot_general(rows, rows, contract, preferred_element_type=F32)
    gram_three = jnp.zeros((rank, rank), F32)
    for owner in range(three_ref.shape[0]):
        rows = three_ref[owner]
        gram_three += lax.dot_general(rows, rows, contract, preferred_element_type=F32)
    row_ids = lax.broadcasted_iota(jnp.int32, (rank, rank), 0)
    col_ids = lax.broadcasted_iota(jnp.int32, (rank, rank), 1)
    unit = (row_ids == col_ids).astype(F32)
    system = gram_two * gram_three + ridge_term * unit
    work = jnp.concatenate([system, unit, jnp.zeros((rank, 128 - 2 * rank), F32)], axis=1)
    below = lax.broadcasted_iota(jnp.int32, (rank, 128), 0)
    scale = jnp.zeros((rank, 128), F32)
    for k in range(rank):
        pivot_row = work[k : k + 1, :]
        inverse = 1.0 / pivot_row[:, k : k + 1]
        scale = jnp.where(below == k, inverse, scale)
        factor = jnp.where(below > k, work[:, k : k + 1] * inverse, 0.0)
        work = work - factor * pivot_row
    lower = work[:, rank : 2 * rank]
    out_ref[...] = lax.dot_general(
        lower,
        lower * scale[:, :rank],
        (((0,), (0,)), ((), ())),
        precision=lax.Precision.HIGHEST,
        preferred_element_type=F32,
    )


def system_inverse(row, own, other, three):
    rank = three.shape[1]
    return pl.pallas_call(
        inverse_kernel,
        in_specs=[SMEM, VMEM, VMEM, VMEM],
        out_specs=VMEM,
        out_shape=jax.ShapeDtypeStruct((rank, rank), F32),
        compiler_params=pltpu.CompilerParams(vmem_limit_bytes=16 * MIB),
        cost_estimate=pl.CostEstimate(flops=8 * MIB, bytes_accessed=16 * MIB, transcendentals=0),
        name="system_inverse",
    )(row, own, other, three)


def solve_kernel(received_ref, inverse_ref, out_ref, side_ref):
    owners, _, edge = received_ref.shape
    rank = inverse_ref.shape[0]
    totals = [jnp.zeros((rank // 8, 8, edge), F32) for _ in range(IB_DEV)]
    for owner in range(owners):
        offsets = received_ref[owner, 2 * rank : 2 * rank + META, :].astype(F32)[None]
        high = received_ref[owner, 0:rank, :].astype(F32)
        low = received_ref[owner, rank : 2 * rank, :].astype(F32)
        rows = (high + low).reshape(rank // 8, 8, edge)
        for offset in range(IB_DEV):
            totals[offset] += jnp.where(offsets == float(offset), rows, 0.0)
    for offset in range(IB_DEV):
        side_ref[:, offset * edge : (offset + 1) * edge] = totals[offset].reshape(rank, edge)
    out_ref[...] = jnp.dot(
        inverse_ref[...],
        side_ref[...],
        precision=lax.Precision.HIGHEST,
        preferred_element_type=F32,
    )


def solve(received, inverse):
    rank = inverse.shape[0]
    edge = received.shape[2]
    return pl.pallas_call(
        solve_kernel,
        in_specs=[VMEM, VMEM],
        out_specs=VMEM,
        out_shape=jax.ShapeDtypeStruct((rank, IB_DEV * edge), F32),
        scratch_shapes=[pltpu.VMEM((rank, IB_DEV * edge), F32)],
        compiler_params=pltpu.CompilerParams(vmem_limit_bytes=16 * MIB),
        name="solve",
    )(received, inverse)


def update(tensor_tiles, tile_mode1, tile_mode2, tile_mode3, factor_mode2, factor_mode3):
    rank, width = factor_mode2.shape
    half = rank // 2
    cols = lax.axis_size("col")
    row = lax.axis_index("row").astype(jnp.int32)
    core = lax.rem(row, 2)
    mine = jnp.where(core == 0, factor_mode2[:half], factor_mode2[half:])
    tiles = pltpu.with_memory_space_constraint(tensor_tiles, pltpu.HBM)
    own = lax.all_to_all(jnp.broadcast_to(mine[None], (cols, half, width)), "col", 0, 0, tiled=True)
    devices = lax.axis_size("row")
    chips = devices // 2
    near, far = [factor_mode3], []
    for distance in range(1, chips):
        shift = [(i, (i + 2 * distance) % devices) for i in range(devices)]
        near.append(lax.ppermute(factor_mode3, "row", shift))
    for distance in range(chips):
        swap = [(i, i ^ 1) for i in range(devices)]
        far.append(lax.ppermute(near[distance], "row", swap))
    three = jnp.stack(near + far)
    swap = [(i, i ^ 1) for i in range(lax.axis_size("row"))]
    other = lax.ppermute(own, "row", swap)
    early = fetch_early(tiles)
    row_id = row[None]
    send = tile_rows(tile_mode1, tile_mode2, tile_mode3, row_id, own, other, three, early, tiles)
    received = lax.all_to_all(send, "col", 0, 0, tiled=True)
    inverse = system_inverse(row_id, own, other, three)
    return solve(received, inverse)


def solution(mesh):
    in_specs = (
        P(("row", "col"), None, None, None),
        P(("row", "col")),
        P(("row", "col")),
        P(("row", "col")),
        P(None, "col"),
        P(None, "row"),
    )
    out_specs = P(None, ("row", "col"))
    return jax.shard_map(update, mesh=mesh, in_specs=in_specs, out_specs=out_specs, check_vma=False)
```

```python
import jax
import jax.numpy as jnp
from jax import lax
from jax.experimental import pallas as pl
from jax.experimental.pallas import tpu as pltpu
from jax.sharding import PartitionSpec as P


IB_DEV = 8
META = 8

ridge_term = 0.5

F32 = jnp.float32
BF16 = jnp.bfloat16
VMEM = pl.BlockSpec(memory_space=pltpu.VMEM)
HBM = pl.BlockSpec(memory_space=pltpu.HBM)
SMEM = pl.BlockSpec(memory_space=pltpu.SMEM)
MIB = 1 << 20


SIDE = 4


def exchange_order(cols):
    lines = cols // SIDE
    return [x * SIDE + z for z in reversed(range(SIDE)) for x in reversed(range(lines))]


def exchange_slot(owner, cols):
    lines = cols // SIDE
    return (SIDE - 1 - lax.rem(owner, SIDE)) * lines + (lines - 1 - lax.div(owner, SIDE))


CHUNKS = 4
EARLY = 2
DEPTH = 3
PARTS = 2


def early_kernel(tiles_ref, out_ref, sems):
    step = out_ref.shape[2]
    copies = [
        pltpu.make_async_copy(
            tiles_ref.at[side, pl.ds(chunk * step, step)],
            out_ref.at[side, chunk],
            sems.at[side, chunk],
        )
        for chunk in range(EARLY)
        for side in range(2)
    ]
    for copy in copies:
        copy.start()
    for copy in copies:
        copy.wait()


def fetch_early(tiles):
    edge = tiles.shape[1]
    return pl.pallas_call(
        early_kernel,
        in_specs=[HBM],
        out_specs=VMEM,
        out_shape=jax.ShapeDtypeStruct((2, EARLY, edge // CHUNKS, edge, edge), BF16),
        scratch_shapes=[pltpu.SemaphoreType.DMA((2, EARLY))],
        compiler_params=pltpu.CompilerParams(vmem_limit_bytes=8 * MIB),
        cost_estimate=pl.CostEstimate(flops=0, bytes_accessed=8 * MIB, transcendentals=0),
        name="fetch_early",
    )(tiles)


def half_rows(own, other, first):
    low = jnp.where(first, own, other)
    high = jnp.where(first, other, own)
    return low, high


def near_slot(row, owner, chips):
    distance = lax.rem(lax.div(row, 2) - lax.div(owner, 2) + chips, chips)
    return distance + chips * lax.rem(row + owner, 2)


def rows_kernel(
    mode1_ref,
    mode2_ref,
    mode3_ref,
    row_id_ref,
    own_ref,
    other_ref,
    three_ref,
    early_ref,
    tiles_ref,
    send_ref,
    weight_ref,
    tile_ref,
    row_ref,
    sems,
):
    tile_count, edge = tiles_ref.shape[:2]
    step = edge // CHUNKS
    steps = [(pair, chunk) for pair in range(tile_count // 2) for chunk in range(CHUNKS)]
    late = steps[EARLY:]

    def copies(number):
        pair, chunk = late[number]
        return [
            pltpu.make_async_copy(
                tiles_ref.at[2 * pair + side, pl.ds(chunk * step, step)],
                tile_ref.at[number, side],
                sems.at[number, side],
            )
            for side in range(2)
        ]

    for number in range(DEPTH):
        for copy in copies(number):
            copy.start()

    @pl.when(row_id_ref[0] >= 0)
    def _():
        fill_rows(
            mode1_ref,
            mode2_ref,
            mode3_ref,
            row_id_ref,
            own_ref,
            other_ref,
            three_ref,
            early_ref,
            send_ref,
            weight_ref,
            tile_ref,
            row_ref,
            steps,
            late,
            copies,
        )


def fill_rows(
    mode1_ref,
    mode2_ref,
    mode3_ref,
    row_id_ref,
    own_ref,
    other_ref,
    three_ref,
    early_ref,
    send_ref,
    weight_ref,
    tile_ref,
    row_ref,
    steps,
    late,
    copies,
):
    owners, half, width = own_ref.shape
    rank = 2 * half
    edge = tile_ref.shape[-1]
    step = tile_ref.shape[2]
    pairs = weight_ref.shape[0]
    per_owner = width // edge

    def place(block):
        start = pl.multiple_of(lax.rem(block, per_owner) * edge, edge)
        return lax.div(block, per_owner), pl.ds(start, edge)

    first = lax.rem(row_id_ref[0], 2) == 0
    send_ref[...] = jnp.zeros_like(send_ref)
    weight_ref[...] = jnp.zeros_like(weight_ref)
    factors = []
    for pair in range(pairs):
        parts = []
        for side in range(2):
            owner, span = place(mode3_ref[2 * pair + side])
            owner = near_slot(row_id_ref[0], owner, three_ref.shape[0] // 2)
            weight_ref[pair, side * rank : (side + 1) * rank, side * edge : (side + 1) * edge] = (
                three_ref[owner, :, span]
            )
            owner, span = place(mode2_ref[2 * pair + side])
            owner = exchange_slot(owner, owners)
            own = own_ref[owner, :, span].astype(F32)
            other = other_ref[owner, :, span].astype(F32)
            parts.extend(half_rows(own, other, first))
        parts.append(jnp.zeros((128 - 2 * rank, edge), F32))
        factors.append(jnp.concatenate(parts, axis=0).T.reshape(1, edge // 8, 8, 128))

    part = step // PARTS
    for number, (pair, chunk) in enumerate(steps):
        if number >= EARLY:
            late_number = number - EARLY
            for copy in copies(late_number):
                copy.wait()
            if late_number + DEPTH < len(late):
                for copy in copies(late_number + DEPTH):
                    copy.start()
        for index in range(PARTS):
            inner = slice(index * part, (index + 1) * part)
            if number < EARLY:
                sides = [early_ref[side, chunk, inner] for side in range(2)]
            else:
                sides = [tile_ref[late_number, side, inner] for side in range(2)]
            both = jnp.concatenate(sides, axis=-1).reshape(part * edge, 2 * edge)
            mid = lax.dot_general(
                both, weight_ref[pair], (((1,), (1,)), ((), ())), preferred_element_type=F32
            )
            terms = mid.reshape(part, edge // 8, 8, 128) * factors[pair]
            while terms.shape[1] > 1:
                terms = terms.reshape(part, terms.shape[1] // 2, 2, 8, 128)
                terms = terms[:, :, 0] + terms[:, :, 1]
            start = chunk * step + index * part
            row_ref[start : start + part, :] = jnp.sum(terms.reshape(part, 8, 128), axis=1)
        if chunk == CHUNKS - 1:
            flipped = row_ref[...].T
            for side in range(2):
                block = mode1_ref[2 * pair + side]
                slot = exchange_slot(lax.rem(lax.div(block, IB_DEV), owners), owners)
                offset = lax.rem(block, IB_DEV).astype(F32)
                rows = flipped[side * rank : (side + 1) * rank, :]
                high = rows.astype(BF16)
                send_ref[slot, 0:rank, :] = high
                send_ref[slot, rank : 2 * rank, :] = (rows - high.astype(F32)).astype(BF16)
                send_ref[slot, 2 * rank : 2 * rank + META, :] = jnp.full(
                    (META, edge), offset, F32
                ).astype(BF16)


def tile_rows(mode1, mode2, mode3, row, own, other, three, early, tiles):
    owners, half, _ = own.shape
    tile_count, edge = tiles.shape[:2]
    late = tile_count // 2 * CHUNKS - EARLY
    return pl.pallas_call(
        rows_kernel,
        in_specs=[SMEM] * 4 + [VMEM] * 4 + [HBM],
        out_specs=VMEM,
        out_shape=jax.ShapeDtypeStruct((owners, 4 * half + META, edge), BF16),
        scratch_shapes=[
            pltpu.VMEM((tile_count // 2, 128, 2 * edge), BF16),
            pltpu.VMEM((late, 2, edge // CHUNKS, edge, edge), BF16),
            pltpu.VMEM((edge, 128), F32),
            pltpu.SemaphoreType.DMA((late, 2)),
        ],
        compiler_params=pltpu.CompilerParams(vmem_limit_bytes=32 * MIB),
        cost_estimate=pl.CostEstimate(
            flops=tile_count * edge * edge * 256 * 256, bytes_accessed=16 * MIB, transcendentals=0
        ),
        name="tile_rows",
    )(mode1, mode2, mode3, row, own, other, three, early, tiles)


def inverse_kernel(row_id_ref, own_ref, other_ref, three_ref, out_ref):
    owners, half, _ = own_ref.shape
    rank = 2 * half
    first = lax.rem(row_id_ref[0], 2) == 0
    contract = (((1,), (1,)), ((), ()))
    gram_two = jnp.zeros((rank, rank), F32)
    for owner in range(owners):
        low, high = half_rows(own_ref[owner].astype(F32), other_ref[owner].astype(F32), first)
        rows = jnp.concatenate([low, high], axis=0).astype(BF16)
        gram_two += lax.dot_general(rows, rows, contract, preferred_element_type=F32)
    gram_three = jnp.zeros((rank, rank), F32)
    for owner in range(three_ref.shape[0]):
        rows = three_ref[owner]
        gram_three += lax.dot_general(rows, rows, contract, preferred_element_type=F32)
    row_ids = lax.broadcasted_iota(jnp.int32, (rank, rank), 0)
    col_ids = lax.broadcasted_iota(jnp.int32, (rank, rank), 1)
    unit = (row_ids == col_ids).astype(F32)
    system = gram_two * gram_three + ridge_term * unit
    work = jnp.concatenate([system, unit, jnp.zeros((rank, 128 - 2 * rank), F32)], axis=1)
    below = lax.broadcasted_iota(jnp.int32, (rank, 128), 0)
    scale = jnp.zeros((rank, 128), F32)
    for k in range(rank):
        pivot_row = work[k : k + 1, :]
        inverse = 1.0 / pivot_row[:, k : k + 1]
        scale = jnp.where(below == k, inverse, scale)
        factor = jnp.where(below > k, work[:, k : k + 1] * inverse, 0.0)
        work = work - factor * pivot_row
    lower = work[:, rank : 2 * rank]
    out_ref[...] = lax.dot_general(
        lower,
        lower * scale[:, :rank],
        (((0,), (0,)), ((), ())),
        precision=lax.Precision.HIGHEST,
        preferred_element_type=F32,
    )


def system_inverse(row, own, other, three):
    rank = three.shape[1]
    return pl.pallas_call(
        inverse_kernel,
        in_specs=[SMEM, VMEM, VMEM, VMEM],
        out_specs=VMEM,
        out_shape=jax.ShapeDtypeStruct((rank, rank), F32),
        compiler_params=pltpu.CompilerParams(vmem_limit_bytes=16 * MIB),
        cost_estimate=pl.CostEstimate(flops=8 * MIB, bytes_accessed=16 * MIB, transcendentals=0),
        name="system_inverse",
    )(row, own, other, three)


def solve_kernel(received_ref, inverse_ref, out_ref, side_ref):
    owners, _, edge = received_ref.shape
    rank = inverse_ref.shape[0]
    totals = [jnp.zeros((rank // 8, 8, edge), F32) for _ in range(IB_DEV)]
    for owner in range(owners):
        offsets = received_ref[owner, 2 * rank : 2 * rank + META, :].astype(F32)[None]
        high = received_ref[owner, 0:rank, :].astype(F32)
        low = received_ref[owner, rank : 2 * rank, :].astype(F32)
        rows = (high + low).reshape(rank // 8, 8, edge)
        for offset in range(IB_DEV):
            totals[offset] += jnp.where(offsets == float(offset), rows, 0.0)
    for offset in range(IB_DEV):
        side_ref[:, offset * edge : (offset + 1) * edge] = totals[offset].reshape(rank, edge)
    out_ref[...] = jnp.dot(
        inverse_ref[...],
        side_ref[...],
        precision=lax.Precision.HIGHEST,
        preferred_element_type=F32,
    )


def solve(received, inverse):
    rank = inverse.shape[0]
    edge = received.shape[2]
    return pl.pallas_call(
        solve_kernel,
        in_specs=[VMEM, VMEM],
        out_specs=VMEM,
        out_shape=jax.ShapeDtypeStruct((rank, IB_DEV * edge), F32),
        scratch_shapes=[pltpu.VMEM((rank, IB_DEV * edge), F32)],
        compiler_params=pltpu.CompilerParams(vmem_limit_bytes=16 * MIB),
        name="solve",
    )(received, inverse)


def update(tensor_tiles, tile_mode1, tile_mode2, tile_mode3, factor_mode2, factor_mode3):
    rank, width = factor_mode2.shape
    half = rank // 2
    cols = lax.axis_size("col")
    row = lax.axis_index("row").astype(jnp.int32)
    core = lax.rem(row, 2)
    mine = jnp.where(core == 0, factor_mode2[:half], factor_mode2[half:])
    tiles = pltpu.with_memory_space_constraint(tensor_tiles, pltpu.HBM)
    own = lax.all_to_all(
        jnp.broadcast_to(mine[None], (cols, half, width)),
        "col",
        0,
        0,
        tiled=True,
        axis_index_groups=[exchange_order(cols)],
    )
    devices = lax.axis_size("row")
    chips = devices // 2
    near, far = [factor_mode3], []
    for distance in range(1, chips):
        shift = [(i, (i + 2 * distance) % devices) for i in range(devices)]
        near.append(lax.ppermute(factor_mode3, "row", shift))
    for distance in range(chips):
        swap = [(i, i ^ 1) for i in range(devices)]
        far.append(lax.ppermute(near[distance], "row", swap))
    three = jnp.stack(near + far)
    swap = [(i, i ^ 1) for i in range(lax.axis_size("row"))]
    other = lax.ppermute(own, "row", swap)
    early = fetch_early(tiles)
    row_id = row[None]
    send = tile_rows(tile_mode1, tile_mode2, tile_mode3, row_id, own, other, three, early, tiles)
    received = lax.all_to_all(
        send, "col", 0, 0, tiled=True, axis_index_groups=[exchange_order(cols)]
    )
    inverse = system_inverse(row_id, own, other, three)
    return solve(received, inverse)


def solution(mesh):
    in_specs = (
        P(("row", "col"), None, None, None),
        P(("row", "col")),
        P(("row", "col")),
        P(("row", "col")),
        P(None, "col"),
        P(None, "row"),
    )
    out_specs = P(None, ("row", "col"))
    return jax.shard_map(update, mesh=mesh, in_specs=in_specs, out_specs=out_specs, check_vma=False)
```

```python
import jax
import jax.numpy as jnp
from jax import lax
from jax.experimental import pallas as pl
from jax.experimental.pallas import tpu as pltpu
from jax.sharding import PartitionSpec as P


IB_DEV = 8
META = 8

ridge_term = 0.5

F32 = jnp.float32
BF16 = jnp.bfloat16
VMEM = pl.BlockSpec(memory_space=pltpu.VMEM)
HBM = pl.BlockSpec(memory_space=pltpu.HBM)
SMEM = pl.BlockSpec(memory_space=pltpu.SMEM)
MIB = 1 << 20


SIDE = 4


def exchange_order(cols):
    lines = cols // SIDE
    return [x * SIDE + z for z in reversed(range(SIDE)) for x in reversed(range(lines))]


def exchange_slot(owner, cols):
    lines = cols // SIDE
    return (SIDE - 1 - lax.rem(owner, SIDE)) * lines + (lines - 1 - lax.div(owner, SIDE))


CHUNKS = 4
EARLY = 2
DEPTH = 3
PARTS = 2


def early_kernel(tiles_ref, out_ref, sems):
    step = out_ref.shape[2]
    copies = [
        pltpu.make_async_copy(
            tiles_ref.at[side, pl.ds(chunk * step, step)],
            out_ref.at[side, chunk],
            sems.at[side, chunk],
        )
        for chunk in range(EARLY)
        for side in range(2)
    ]
    for copy in copies:
        copy.start()
    for copy in copies:
        copy.wait()


def fetch_early(tiles):
    edge = tiles.shape[1]
    return pl.pallas_call(
        early_kernel,
        in_specs=[HBM],
        out_specs=VMEM,
        out_shape=jax.ShapeDtypeStruct((2, EARLY, edge // CHUNKS, edge, edge), BF16),
        scratch_shapes=[pltpu.SemaphoreType.DMA((2, EARLY))],
        compiler_params=pltpu.CompilerParams(vmem_limit_bytes=8 * MIB),
        cost_estimate=pl.CostEstimate(flops=0, bytes_accessed=8 * MIB, transcendentals=0),
        name="fetch_early",
    )(tiles)


def half_rows(own, other, first):
    low = jnp.where(first, own, other)
    high = jnp.where(first, other, own)
    return low, high


def near_slot(row, owner, chips):
    distance = lax.rem(lax.div(row, 2) - lax.div(owner, 2) + chips, chips)
    return distance + chips * lax.rem(row + owner, 2)


def rows_kernel(
    mode1_ref,
    mode2_ref,
    mode3_ref,
    row_id_ref,
    own_ref,
    other_ref,
    three_ref,
    early_ref,
    tiles_ref,
    send_ref,
    weight_ref,
    tile_ref,
    row_ref,
    sems,
):
    tile_count, edge = tiles_ref.shape[:2]
    step = edge // CHUNKS
    steps = [(pair, chunk) for pair in range(tile_count // 2) for chunk in range(CHUNKS)]
    late = steps[EARLY:]

    def copies(number):
        pair, chunk = late[number]
        return [
            pltpu.make_async_copy(
                tiles_ref.at[2 * pair + side, pl.ds(chunk * step, step)],
                tile_ref.at[number, side],
                sems.at[number, side],
            )
            for side in range(2)
        ]

    for number in range(DEPTH):
        for copy in copies(number):
            copy.start()

    @pl.when(row_id_ref[0] >= 0)
    def _():
        fill_rows(
            mode1_ref,
            mode2_ref,
            mode3_ref,
            row_id_ref,
            own_ref,
            other_ref,
            three_ref,
            early_ref,
            send_ref,
            weight_ref,
            tile_ref,
            row_ref,
            steps,
            late,
            copies,
        )


def fill_rows(
    mode1_ref,
    mode2_ref,
    mode3_ref,
    row_id_ref,
    own_ref,
    other_ref,
    three_ref,
    early_ref,
    send_ref,
    weight_ref,
    tile_ref,
    row_ref,
    steps,
    late,
    copies,
):
    owners, half, width = own_ref.shape
    rank = 2 * half
    edge = tile_ref.shape[-1]
    step = tile_ref.shape[2]
    pairs = weight_ref.shape[0]
    per_owner = width // edge

    def place(block):
        start = pl.multiple_of(lax.rem(block, per_owner) * edge, edge)
        return lax.div(block, per_owner), pl.ds(start, edge)

    first = lax.rem(row_id_ref[0], 2) == 0
    send_ref[...] = jnp.zeros_like(send_ref)
    weight_ref[...] = jnp.zeros_like(weight_ref)
    factors = []
    for pair in range(pairs):
        parts = []
        for side in range(2):
            owner, span = place(mode3_ref[2 * pair + side])
            owner = near_slot(row_id_ref[0], owner, three_ref.shape[0] // 2)
            weight_ref[pair, side * rank : (side + 1) * rank, side * edge : (side + 1) * edge] = (
                three_ref[owner, :, span]
            )
            owner, span = place(mode2_ref[2 * pair + side])
            owner = exchange_slot(owner, owners)
            own = own_ref[owner, :, span].astype(F32)
            other = other_ref[owner, :, span].astype(F32)
            parts.extend(half_rows(own, other, first))
        parts.append(jnp.zeros((128 - 2 * rank, edge), F32))
        factors.append(jnp.concatenate(parts, axis=0).T.reshape(1, edge // 8, 8, 128))

    part = step // PARTS
    for number, (pair, chunk) in enumerate(steps):
        if number >= EARLY:
            late_number = number - EARLY
            for copy in copies(late_number):
                copy.wait()
            if late_number + DEPTH < len(late):
                for copy in copies(late_number + DEPTH):
                    copy.start()
        for index in range(PARTS):
            inner = slice(index * part, (index + 1) * part)
            if number < EARLY:
                sides = [early_ref[side, chunk, inner] for side in range(2)]
            else:
                sides = [tile_ref[late_number, side, inner] for side in range(2)]
            both = jnp.concatenate(sides, axis=-1).reshape(part * edge, 2 * edge)
            mid = lax.dot_general(
                both, weight_ref[pair], (((1,), (1,)), ((), ())), preferred_element_type=F32
            )
            terms = mid.reshape(part, edge // 8, 8, 128) * factors[pair]
            while terms.shape[1] > 1:
                terms = terms.reshape(part, terms.shape[1] // 2, 2, 8, 128)
                terms = terms[:, :, 0] + terms[:, :, 1]
            start = chunk * step + index * part
            row_ref[start : start + part, :] = jnp.sum(terms.reshape(part, 8, 128), axis=1)
        if chunk == CHUNKS - 1:
            flipped = row_ref[...].T
            for side in range(2):
                block = mode1_ref[2 * pair + side]
                slot = exchange_slot(lax.rem(lax.div(block, IB_DEV), owners), owners)
                offset = lax.rem(block, IB_DEV).astype(F32)
                rows = flipped[side * rank : (side + 1) * rank, :]
                high = rows.astype(BF16)
                send_ref[slot, 0:rank, :] = high
                send_ref[slot, rank : 2 * rank, :] = (rows - high.astype(F32)).astype(BF16)
                send_ref[slot, 2 * rank : 2 * rank + META, :] = jnp.full(
                    (META, edge), offset, F32
                ).astype(BF16)


def tile_rows(mode1, mode2, mode3, row, own, other, three, early, tiles):
    owners, half, _ = own.shape
    tile_count, edge = tiles.shape[:2]
    late = tile_count // 2 * CHUNKS - EARLY
    return pl.pallas_call(
        rows_kernel,
        in_specs=[SMEM] * 4 + [VMEM] * 4 + [HBM],
        out_specs=VMEM,
        out_shape=jax.ShapeDtypeStruct((owners, 4 * half + META, edge), BF16),
        scratch_shapes=[
            pltpu.VMEM((tile_count // 2, 128, 2 * edge), BF16),
            pltpu.VMEM((late, 2, edge // CHUNKS, edge, edge), BF16),
            pltpu.VMEM((edge, 128), F32),
            pltpu.SemaphoreType.DMA((late, 2)),
        ],
        compiler_params=pltpu.CompilerParams(vmem_limit_bytes=32 * MIB),
        cost_estimate=pl.CostEstimate(
            flops=tile_count * edge * edge * 256 * 256, bytes_accessed=16 * MIB, transcendentals=0
        ),
        name="tile_rows",
    )(mode1, mode2, mode3, row, own, other, three, early, tiles)


def inverse_kernel(row_id_ref, own_ref, other_ref, three_ref, out_ref):
    owners, half, _ = own_ref.shape
    rank = 2 * half
    first = lax.rem(row_id_ref[0], 2) == 0
    contract = (((1,), (1,)), ((), ()))
    gram_two = jnp.zeros((rank, rank), F32)
    for owner in range(owners):
        low, high = half_rows(own_ref[owner].astype(F32), other_ref[owner].astype(F32), first)
        rows = jnp.concatenate([low, high], axis=0).astype(BF16)
        gram_two += lax.dot_general(rows, rows, contract, preferred_element_type=F32)
    gram_three = jnp.zeros((rank, rank), F32)
    for owner in range(three_ref.shape[0]):
        rows = three_ref[owner]
        gram_three += lax.dot_general(rows, rows, contract, preferred_element_type=F32)
    row_ids = lax.broadcasted_iota(jnp.int32, (rank, rank), 0)
    col_ids = lax.broadcasted_iota(jnp.int32, (rank, rank), 1)
    unit = (row_ids == col_ids).astype(F32)
    system = gram_two * gram_three + ridge_term * unit
    work = jnp.concatenate([system, unit, jnp.zeros((rank, 128 - 2 * rank), F32)], axis=1)
    below = lax.broadcasted_iota(jnp.int32, (rank, 128), 0)
    scale = jnp.zeros((rank, 128), F32)
    for k in range(rank):
        pivot_row = work[k : k + 1, :]
        inverse = 1.0 / pivot_row[:, k : k + 1]
        scale = jnp.where(below == k, inverse, scale)
        factor = jnp.where(below > k, work[:, k : k + 1] * inverse, 0.0)
        work = work - factor * pivot_row
    lower = work[:, rank : 2 * rank]
    out_ref[...] = lax.dot_general(
        lower,
        lower * scale[:, :rank],
        (((0,), (0,)), ((), ())),
        precision=lax.Precision.HIGHEST,
        preferred_element_type=F32,
    )


def system_inverse(row, own, other, three):
    rank = three.shape[1]
    return pl.pallas_call(
        inverse_kernel,
        in_specs=[SMEM, VMEM, VMEM, VMEM],
        out_specs=VMEM,
        out_shape=jax.ShapeDtypeStruct((rank, rank), F32),
        compiler_params=pltpu.CompilerParams(vmem_limit_bytes=16 * MIB),
        cost_estimate=pl.CostEstimate(flops=8 * MIB, bytes_accessed=16 * MIB, transcendentals=0),
        name="system_inverse",
    )(row, own, other, three)


def parts_of(value):
    parts = []
    for _ in range(3):
        part = value.astype(BF16)
        parts.append(part)
        value = value - part.astype(F32)
    return parts


def solve_kernel(received_ref, inverse_ref, out_ref, side_ref):
    owners, _, edge = received_ref.shape
    rank = inverse_ref.shape[0]
    totals = [jnp.zeros((rank // 8, 8, edge), F32) for _ in range(IB_DEV)]
    for owner in range(owners):
        offsets = received_ref[owner, 2 * rank : 2 * rank + META, :].astype(F32)[None]
        high = received_ref[owner, 0:rank, :].astype(F32)
        low = received_ref[owner, rank : 2 * rank, :].astype(F32)
        rows = (high + low).reshape(rank // 8, 8, edge)
        for offset in range(IB_DEV):
            totals[offset] += jnp.where(offsets == float(offset), rows, 0.0)
    for offset in range(IB_DEV):
        side_ref[:, offset * edge : (offset + 1) * edge] = totals[offset].reshape(rank, edge)
    left, right = parts_of(inverse_ref[...]), parts_of(side_ref[...])
    pairs = [(0, 0), (0, 1), (1, 0), (1, 1), (0, 2), (2, 0)]
    out_ref[...] = jnp.dot(
        jnp.concatenate([left[a] for a, _ in pairs], axis=1),
        jnp.concatenate([right[b] for _, b in pairs], axis=0),
        preferred_element_type=F32,
    )


def solve(received, inverse):
    rank = inverse.shape[0]
    edge = received.shape[2]
    return pl.pallas_call(
        solve_kernel,
        in_specs=[VMEM, VMEM],
        out_specs=VMEM,
        out_shape=jax.ShapeDtypeStruct((rank, IB_DEV * edge), F32),
        scratch_shapes=[pltpu.VMEM((rank, IB_DEV * edge), F32)],
        compiler_params=pltpu.CompilerParams(vmem_limit_bytes=16 * MIB),
        name="solve",
    )(received, inverse)


def update(tensor_tiles, tile_mode1, tile_mode2, tile_mode3, factor_mode2, factor_mode3):
    rank, width = factor_mode2.shape
    half = rank // 2
    cols = lax.axis_size("col")
    row = lax.axis_index("row").astype(jnp.int32)
    core = lax.rem(row, 2)
    mine = jnp.where(core == 0, factor_mode2[:half], factor_mode2[half:])
    tiles = pltpu.with_memory_space_constraint(tensor_tiles, pltpu.HBM)
    own = lax.all_to_all(
        jnp.broadcast_to(mine[None], (cols, half, width)),
        "col",
        0,
        0,
        tiled=True,
        axis_index_groups=[exchange_order(cols)],
    )
    devices = lax.axis_size("row")
    chips = devices // 2
    near, far = [factor_mode3], []
    for distance in range(1, chips):
        shift = [(i, (i + 2 * distance) % devices) for i in range(devices)]
        near.append(lax.ppermute(factor_mode3, "row", shift))
    for distance in range(chips):
        swap = [(i, i ^ 1) for i in range(devices)]
        far.append(lax.ppermute(near[distance], "row", swap))
    three = jnp.stack(near + far)
    swap = [(i, i ^ 1) for i in range(lax.axis_size("row"))]
    other = lax.ppermute(own, "row", swap)
    early = fetch_early(tiles)
    row_id = row[None]
    send = tile_rows(tile_mode1, tile_mode2, tile_mode3, row_id, own, other, three, early, tiles)
    received = lax.all_to_all(
        send, "col", 0, 0, tiled=True, axis_index_groups=[exchange_order(cols)]
    )
    inverse = system_inverse(row_id, own, other, three)
    return solve(received, inverse)


def solution(mesh):
    in_specs = (
        P(("row", "col"), None, None, None),
        P(("row", "col")),
        P(("row", "col")),
        P(("row", "col")),
        P(None, "col"),
        P(None, "row"),
    )
    out_specs = P(None, ("row", "col"))
    return jax.shard_map(update, mesh=mesh, in_specs=in_specs, out_specs=out_specs, check_vma=False)
```
